128 devices in a mesh: group: 4 (over z), batch: 32 (over x, y, core).
Axes of the slice: x: 4, y: 4, z: 4, core: 2. Of those that a mesh axis runs over, the one named last changes fastest.
Arguments:
- embeds: bfloat16 [262144, 256], P(('group', 'batch')), may hold values from -6 to 6
- out_grad: bfloat16 [262144, 256], P(('group', 'batch')), may hold values from -48 to 48
- w_query: bfloat16 [256, 256], replicated, may hold values from -0.375 to 0.375
- w_key: bfloat16 [256, 256], replicated, may hold values from -0.375 to 0.375
- w_value: bfloat16 [256, 256], replicated, may hold values from -0.375 to 0.375
- lengths: int32 [512], P(('group', 'batch')), may hold values from 1 to 512, as said below
- item_rows: int32 [262144], P(('group', 'batch')), may hold values from 0 to 8191, as said below
- tile_owner: int32 [2048], P(('group', 'batch')), may hold values from 0 to 3, as said below
Outputs:
- table_grad: float32 [32768, 256], P(('group', 'batch'))
The draws below stay inside these ranges and needn't reach their ends.
Inputs may be any that keep to these rules, and one draw needn't show every extreme that they name: `lengths`: a history's live tokens are its first positions; in every draw some history has exactly 512 live tokens. `tile_owner`: among the first 8 tiles of each device's own tiles, and among the last 8, every group owns exactly 2 tiles. `item_rows`: of the 128 tokens of each tile, at most 8 have rows r with the same r // 256, and in every tile some value of r // 256 is taken by exactly 8 tokens.
All inputs are finite; a program needn't handle non-finite values.
Results may differ from the reference program's by a relative error of at most 0.0024.
The reference program's roundings to bfloat16 on the way (of `attend`, `value_grad`, `score_grad` and `token_grad`) count: a program that leaves them out, or rounds other values in their place, can miss the bound.
Values may be sent and summed in bfloat16 or wider, within the bound.
A program may use at most 64 MiB of HBM per device.

```python
import math
import jax
import jax.numpy as jnp
from jax import lax

D = 256
HEADS = 2
DH = 128
TILE = 128
SEQ_LEN = 512
SEQ_DEV = 4
ROWS_DEV = 256
GROUPS = 4
BATCHES = 32
TILE_MOST = 8
ROWS_GRP = 8192
ITEMS = 32768
SEQS = 512
TOKENS = 262144
TILES_DEV = 16
TILES = 2048


def draw_lengths(key, part):
    stream = jax.random.fold_in(key, 11)
    index = jnp.arange(SEQS, dtype=jnp.int32)
    device = index // SEQ_DEV
    column = device % BATCHES
    upper = SEQ_LEN * (BATCHES - 1 + 2 * column) // (3 * (BATCHES - 1))
    lower = jnp.maximum(upper // 2, 1)
    drawn = jax.random.randint(stream, (SEQS,), lower, upper + 1)
    longest = (column == BATCHES - 1) & (index % SEQ_DEV == SEQ_DEV - 1)
    return jnp.where(longest, SEQ_LEN, drawn).astype(jnp.int32)


def draw_tile_owner(key, part):
    stream = jax.random.fold_in(key, 23)
    half_tiles = TILES_DEV // 2
    block_count = TILES // half_tiles
    raw_scores = jax.random.randint(stream, (block_count, half_tiles), 0, 1 << 20)
    scores = raw_scores * half_tiles + jnp.arange(half_tiles, dtype=jnp.int32)[None, :]
    ranking = jnp.argsort(jnp.argsort(scores, axis=1), axis=1)
    return (ranking % GROUPS).reshape(TILES).astype(jnp.int32)


def draw_item_rows(key, part):
    owners = draw_tile_owner(key, part)
    tile_index = jnp.arange(TILES, dtype=jnp.int32)
    column = tile_index // TILES_DEV % BATCHES
    offsets = jax.random.randint(jax.random.fold_in(key, 31), (GROUPS,), 0, BATCHES)
    hottest = (column + offsets[owners]) % BATCHES
    pool_size = (BATCHES - 1) * TILE_MOST
    counter = jnp.arange(pool_size, dtype=jnp.int32)
    pool = (hottest[:, None] + 1 + counter[None, :] // TILE_MOST) % BATCHES
    pool_scores = jax.random.randint(jax.random.fold_in(key, 37), (TILES, pool_size), 0, 1 << 20) * pool_size + counter[None, :]
    pool_order = jnp.argsort(pool_scores, axis=1)
    picked = jnp.take_along_axis(pool, pool_order, axis=1)[:, :TILE - TILE_MOST]
    hot_block = jnp.broadcast_to(hottest[:, None], (TILES, TILE_MOST))
    joined = jnp.concatenate([hot_block, picked], axis=1)
    place_scores = jax.random.randint(jax.random.fold_in(key, 41), (TILES, TILE), 0, 1 << 20) * TILE + jnp.arange(TILE, dtype=jnp.int32)[None, :]
    place_order = jnp.argsort(place_scores, axis=1)
    holder = jnp.take_along_axis(joined, place_order, axis=1)
    drawn = jax.random.randint(jax.random.fold_in(key, 43), (TILES, TILE), 0, ROWS_DEV)
    local_row = drawn * drawn // ROWS_DEV
    return (holder * ROWS_DEV + local_row).reshape(TOKENS).astype(jnp.int32)


def levels(stream_key, dims, split, least, top_value):
    gain = 1.0
    for dim, shards_of in split:
        steps = jax.random.uniform(jax.random.fold_in(jax.random.fold_in(stream_key, 6), dim), (shards_of,), jnp.float32, least / len(split), top_value / len(split))
        gain = gain * jnp.repeat(jnp.exp(steps), dims[dim] // shards_of).reshape((-1,) + (1,) * (len(dims) - 1 - dim))
    return gain


def scatter_about(own_key, extent, spread, most, cuts=(), kind=jnp.bfloat16):
    loudness = levels(own_key, extent, cuts, -0.22, 0.18) if cuts else 1.0
    values = jax.random.normal(own_key, extent, jnp.float32) * spread * loudness
    return jnp.minimum(jnp.maximum(values, -most), most).astype(kind)


def setup_inputs(seed: int = 0) -> dict:
    splits = jax.random.split(jax.random.key(seed), 9)
    return {
        "embeds": scatter_about(splits[0], (TOKENS, D), 1.0, 6.0, ((0, 128),)),
        "out_grad": scatter_about(splits[1], (TOKENS, D), 8.0, 48.0, ((0, 128),)),
        "w_query": scatter_about(splits[2], (D, D), D ** -0.5, 0.375),
        "w_key": scatter_about(splits[3], (D, D), D ** -0.5, 0.375),
        "w_value": scatter_about(splits[4], (D, D), D ** -0.5, 0.375),
        "lengths": draw_lengths(jax.random.fold_in(splits[8], 71), 0),
        "item_rows": draw_item_rows(jax.random.fold_in(splits[8], 71), 0),
        "tile_owner": draw_tile_owner(jax.random.fold_in(splits[8], 71), 0),
    }


def sequence_grads(query, key_rows, value, grad_out, count, w_query, w_key, w_value):
    span = query.shape[0]
    position = lax.broadcasted_iota(jnp.int32, (span, span), 0)
    other = lax.broadcasted_iota(jnp.int32, (span, span), 1)
    live = ((other <= position) & (position < count)).astype(jnp.float32)
    weight = live / count.astype(jnp.float32)
    scale = 1.0 / math.sqrt(query.shape[2])
    highest = lax.Precision.HIGHEST
    query_f = query.astype(jnp.float32)
    key_f = key_rows.astype(jnp.float32)
    value_f = value.astype(jnp.float32)
    grad_f = grad_out.astype(jnp.float32)
    scores = jnp.einsum('ihd,jhd->hij', query_f, key_f, precision=highest) * scale
    sigma = jax.nn.sigmoid(scores)
    attend = (scores * sigma * weight).astype(jnp.bfloat16)
    value_grad = jnp.einsum('hij,ihd->jhd', attend.astype(jnp.float32), grad_f, precision=highest).astype(jnp.bfloat16)
    attend_grad = jnp.einsum('ihd,jhd->hij', grad_f, value_f, precision=highest)
    score_grad = (attend_grad * weight * sigma * (1.0 + scores * (1.0 - sigma))).astype(jnp.bfloat16)
    score_f = score_grad.astype(jnp.float32)
    query_grad = (jnp.einsum('hij,jhd->ihd', score_f, key_f, precision=highest) * scale).astype(jnp.bfloat16)
    key_grad = (jnp.einsum('hij,ihd->jhd', score_f, query_f, precision=highest) * scale).astype(jnp.bfloat16)
    width = w_query.shape[0]
    token = jnp.dot(query_grad.reshape(span, width), w_query.T, preferred_element_type=jnp.float32)
    token = token + jnp.dot(key_grad.reshape(span, width), w_key.T, preferred_element_type=jnp.float32)
    token = token + jnp.dot(value_grad.reshape(span, width), w_value.T, preferred_element_type=jnp.float32)
    return token.astype(jnp.bfloat16)

def reference(embeds, out_grad, w_query, w_key, w_value, lengths, item_rows, tile_owner):

    def project(weight_matrix):
        return jnp.dot(embeds, weight_matrix, preferred_element_type=jnp.float32).astype(jnp.bfloat16).reshape(SEQS, SEQ_LEN, HEADS, DH)
    query = project(w_query)
    key_rows = project(w_key)
    value = project(w_value)
    grad_heads = out_grad.reshape(SEQS, SEQ_LEN, HEADS, DH)

    def one_history(item):
        return sequence_grads(item[0], item[1], item[2], item[3], item[4], w_query, w_key, w_value)
    token_grad = lax.map(one_history, (query, key_rows, value, grad_heads, lengths)).reshape(TOKENS, D)
    table_rows = (jnp.repeat(tile_owner, TILE) * ROWS_GRP + item_rows).astype(jnp.int32)
    summed = jax.ops.segment_sum(token_grad.astype(jnp.float32), table_rows, num_segments=ITEMS)
    live_total = jnp.sum(lengths.astype(jnp.float32))
    return TOKENS / live_total * summed
```

```python
import functools
import math

import jax
import jax.numpy as jnp
from jax import lax
from jax.experimental import pallas as pl
from jax.experimental.pallas import tpu as pltpu
from jax.sharding import PartitionSpec as P

SEQ = 512
TILE = 128
HEAD = 128
BLOCK = 128
ROWS = 256
MESH_ID = pl.DeviceIdType.MESH
F32 = jnp.float32
BF16 = jnp.bfloat16


def dot(a, b, dims):
    return lax.dot_general(a, b, ((dims[:1], dims[1:]), ((), ())), preferred_element_type=F32)


def iota(shape, dim):
    return lax.broadcasted_iota(jnp.int32, shape, dim)


def onehot(rows, index):
    return jnp.where(iota((rows, index.shape[1]), 0) == index, 1.0, 0.0).astype(BF16)


def history(item, len_ref, emb_ref, og_ref, wq_ref, wk_ref, wv_ref, tok_ref):
    span = pl.ds(pl.multiple_of(item * SEQ, SEQ), SEQ)
    count = len_ref[item]
    embeds = emb_ref[span, :]
    grads = og_ref[span, :]
    query = dot(embeds, wq_ref[...], (1, 0)).astype(BF16)
    keys = dot(embeds, wk_ref[...], (1, 0)).astype(BF16)
    value = dot(embeds, wv_ref[...], (1, 0)).astype(BF16)
    scale = 1.0 / math.sqrt(HEAD)
    counts = jnp.full((1, SEQ), count, jnp.int32)
    weight = jnp.where(iota((1, SEQ), 1) < counts, 1.0 / counts.astype(F32), 0.0)
    causal = iota((BLOCK, BLOCK), 1) >= iota((BLOCK, BLOCK), 0)
    query_parts, key_parts, value_parts = [], [], []
    for head in range(2):
        cols = slice(head * HEAD, (head + 1) * HEAD)
        total = [None] * (SEQ // BLOCK)
        key_blocks, value_blocks = [], []
        for block in range(SEQ // BLOCK):
            at = block * BLOCK
            q, g = query[at:, cols], grads[at:, cols]
            k, v = keys[at : at + BLOCK, cols], value[at : at + BLOCK, cols]
            raw = dot(k, q, (1, 1))
            attend_grad = dot(v, g, (1, 1))
            sigma = 0.5 * jnp.tanh(raw * (0.5 * scale)) + 0.5
            diagonal = jnp.where(causal, weight[:, at : at + BLOCK], 0.0)
            if at + BLOCK < SEQ:
                rest = jnp.broadcast_to(weight[:, at + BLOCK :], (BLOCK, SEQ - at - BLOCK))
                diagonal = jnp.concatenate([diagonal, rest], axis=1)
            gated = sigma * diagonal
            attend = (raw * scale) * gated
            score = (attend_grad * (gated + attend * (1.0 - sigma))).astype(BF16)
            value_blocks.append(dot(attend.astype(BF16), g, (1, 0)).astype(BF16))
            key_blocks.append((dot(score, q, (1, 0)) * scale).astype(BF16))
            part = dot(score, k, (0, 0))
            for row in range(block, SEQ // BLOCK):
                piece = part[row * BLOCK - at : (row + 1) * BLOCK - at]
                total[row] = piece if total[row] is None else total[row] + piece
        query_parts.append((jnp.concatenate(total, axis=0) * scale).astype(BF16))
        key_parts.append(jnp.concatenate(key_blocks, axis=0))
        value_parts.append(jnp.concatenate(value_blocks, axis=0))
    token = dot(jnp.concatenate(query_parts, axis=1), wq_ref[...], (1, 1))
    token = token + dot(jnp.concatenate(key_parts, axis=1), wk_ref[...], (1, 1))
    token = token + dot(jnp.concatenate(value_parts, axis=1), wv_ref[...], (1, 1))
    tiles = SEQ // TILE
    tok_ref[pl.ds(item * tiles, tiles)] = token.astype(BF16).reshape(tiles, TILE, 2 * HEAD)


def kernel(
    len_ref, owner_ref, rows_ref, emb_ref, og_ref, wq_ref, wk_ref, wv_ref, out_ref,
    tok, order, m1s, m1r, zs, zr, m2s, m2r, ss, sr, m3s, m3r, acc, ds_, dr, send_sem, recv_sem,
):
    group = lax.axis_index("group")
    batch = lax.axis_index("batch")
    my_x, my_y, my_c = batch // 8, lax.rem(batch // 2, 4), lax.rem(batch, 2)

    def device(dx=0, dy=0, dz=0, dc=0):
        x, y = lax.rem(my_x + dx, 4), lax.rem(my_y + dy, 4)
        return (lax.rem(group + dz, 4), x * 8 + y * 2 + lax.rem(my_c + dc, 2))

    def line(axis, d):
        return device(dx=d // 2, dc=d % 2) if axis == 0 else device(dy=d // 2, dc=d % 2)

    peers = [device(dz=d) for d in (1, 2, 3)]
    peers += [line(0, d) for d in range(1, 8)] + [line(1, d) for d in range(2, 8)]
    barrier = pltpu.get_barrier_semaphore()
    for peer in peers:
        pl.semaphore_signal(barrier, inc=1, device_id=peer, device_id_type=MESH_ID)
    pl.semaphore_wait(barrier, len(peers))

    used = []

    def remote(source, target, peer):
        slot = len(used)
        used.append(slot)
        copy = pltpu.make_async_remote_copy(
            src_ref=source,
            dst_ref=target,
            send_sem=send_sem.at[slot],
            recv_sem=recv_sem.at[slot],
            device_id=peer,
            device_id_type=MESH_ID,
        )
        copy.start()
        return copy

    live = len_ref[0] + len_ref[1] + len_ref[2] + len_ref[3]
    for half in range(2):
        owner = [owner_ref[half * 8 + t] for t in range(8)]
        place = []
        for t in range(8):
            at = 2 * owner[t]
            for other in owner[:t]:
                at = at + jnp.where(other == owner[t], 1, 0)
            place.append(at)
        for p in range(8):
            tile = 0
            for t in range(1, 8):
                tile = tile + jnp.where(place[t] == p, t, 0)
            order[half * 8 + p] = tile + half * 8

    def owned(half, dz, k):
        return order[half * 8 + 2 * lax.rem(group + dz, 4) + k]

    first = []
    for dz in range(4):
        target = m1s.at[dz] if dz else m1r.at[0]
        for half in range(2):
            for k in range(2):
                target[half * 2 + k : half * 2 + k + 1, :] = rows_ref[pl.ds(owned(half, dz, k), 1), :]
        target[4:5, :] = jnp.full((1, TILE), live, jnp.int32)
        target[5:8, :] = jnp.zeros((3, TILE), jnp.int32)
    for dz in range(1, 4):
        first.append(remote(m1s.at[dz], m1r.at[dz], device(dz=dz)))

    def compute(half):
        def step(i, carry):
            history(i, len_ref, emb_ref, og_ref, wq_ref, wk_ref, wv_ref, tok)
            return carry

        lax.fori_loop(half * 2, half * 2 + 2, step, 0)
        copies = []
        for dz in (1, 3, 2):
            for k in range(2):
                zs[half, dz, pl.ds(k * TILE, TILE), :] = tok[owned(half, dz, k)]
            copies.append(remote(zs.at[half, dz], zr.at[half, dz], device(dz=dz)))
        for k in range(2):
            zr[half, 0, pl.ds(k * TILE, TILE), :] = tok[owned(half, 0, k)]
        return copies

    tiles = [compute(0)]

    for copy in first:
        copy.wait()
    heads = jnp.concatenate(
        [m1r[dz, half * 2 + k : half * 2 + k + 1, :] for half in range(2) for dz in range(4) for k in range(2)],
        axis=0,
    )
    holder = heads // ROWS
    local = lax.rem(heads, ROWS)
    before = jnp.where(iota((TILE, TILE), 0) < iota((TILE, TILE), 1), 1.0, 0.0).astype(BF16)
    marks = jnp.concatenate([onehot(32, holder[u : u + 1, :]) for u in range(16)], axis=0)
    earlier = dot(marks, before, (1, 0)) * marks.astype(F32)
    rank = jnp.concatenate(
        [jnp.sum(earlier[u * 32 : (u + 1) * 32], axis=0, keepdims=True) for u in range(16)], axis=0
    ).astype(jnp.int32)
    away_x = lax.rem(holder // 8 + 4 - my_x, 4)
    away_y = lax.rem(lax.rem(holder // 2, 4) + 4 - my_y, 4)
    away_c = lax.rem(lax.rem(holder, 2) + 2 - my_c, 2)
    within = rank + 8 * lax.rem(iota((16, TILE), 0), 2)
    dest = [away_x * 2 + away_c, away_y * 2 + away_c]
    line_row = [away_y, away_x]
    slots = [dest[axis] * 64 + line_row[axis] * 16 + within for axis in range(2)]
    meta_row = [dest[axis] * 8 + line_row[axis] for axis in range(2)]
    meta_lane = within + 16 * (iota((16, TILE), 0) // 2)

    def pair(array, unit):
        return jnp.concatenate([array[2 * unit : 2 * unit + 1, :], array[2 * unit + 1 : 2 * unit + 2, :]], axis=1)

    live_z = m1r[0, 4:5, :] + m1r[1, 4:5, :] + m1r[2, 4:5, :] + m1r[3, 4:5, :]
    live_row = jnp.where(lax.rem(iota((64, TILE), 0), 8) == 4, live_z.astype(F32), 0.0)
    second = [[], []]
    for axis in range(2):
        meta = live_row
        for unit in range(8):
            left = jnp.where(iota((64, 256), 0) == pair(meta_row[axis], unit), pair(local, unit).astype(F32), 0.0)
            meta = meta + dot(left.astype(BF16), onehot(TILE, pair(meta_lane, unit)), (1, 1))
        for d in range(8):
            target = m2s.at[axis, d] if d else m2r.at[axis, 0]
            target[...] = meta[d * 8 : (d + 1) * 8, :]
        for d in range(1, 8):
            second[axis].append(remote(m2s.at[axis, d], m2r.at[axis, d], line(axis, d)))

    tiles.append(compute(1))

    for axis in range(2):
        for copy in second[axis]:
            copy.wait()
    live_x = m2r[0, 0, 4:5, :]
    for d in range(1, 8):
        live_x = live_x + m2r[0, d, 4:5, :]
    live_x = jnp.broadcast_to(live_x, (8, TILE))
    m3r[0] = live_x
    m3s[...] = live_x
    third = [remote(m3s, m3r.at[dy], device(dy=dy)) for dy in (1, 2, 3)]

    slot_copies = []
    for half in range(2):
        for copy in tiles[half]:
            copy.wait()
        for axis in range(2):
            for dz in range(4):
                packed = dot(
                    onehot(512, pair(slots[axis], half * 4 + dz)),
                    zr[half, dz, :, axis * HEAD : (axis + 1) * HEAD],
                    (1, 0),
                ).astype(BF16)
                for d in range(8):
                    target = ss.at[half, axis, d] if d else sr.at[half, axis, 0]
                    for row in range(4):
                        at = d * 64 + row * 16
                        target[row, dz * 16 : (dz + 1) * 16, :] = packed[at : at + 16]
        copies = []
        for d in (2, 6, 4, 3, 7, 5, 1):
            for axis in range(2):
                copies.append(remote(ss.at[half, axis, d], sr.at[half, axis, d], line(axis, d)))
        slot_copies.append(copies)

    low = iota((8, TILE), 1) < 64
    sums = []
    for half in range(2):
        for copy in slot_copies[half]:
            copy.wait()
        for axis in range(2):
            index = []
            for d in range(0, 8, 2):
                a, b = m2r[axis, d], m2r[axis, d + 1]
                if half == 0:
                    index.append(jnp.where(low, a, pltpu.roll(b, 64, 1)))
                else:
                    index.append(jnp.where(low, pltpu.roll(a, 64, 1), b))
            index = jnp.concatenate(index, axis=1).astype(jnp.int32)
            for row in range(4):
                data = sr[half, axis, :, row].reshape(512, HEAD)
                part = dot(onehot(ROWS, index[row : row + 1, :]), data, (1, 0))
                if half == 0:
                    acc[axis, row] = part
                elif row == 0:
                    acc[axis, 0] = acc[axis, 0] + part
                else:
                    ds_[axis, row] = (acc[axis, row] + part).astype(BF16)
                    peer = device(dy=row) if axis == 0 else device(dx=row)
                    sums.append(remote(ds_.at[axis, row], dr.at[axis, row], peer))

    for copy in third:
        copy.wait()
    total_live = m3r[0, 0:1, :] + m3r[1, 0:1, :] + m3r[2, 0:1, :] + m3r[3, 0:1, :]
    factor = float(SEQ * 4 * 128) / total_live
    for copy in sums:
        copy.wait()
    for axis in range(2):
        result = acc[axis, 0]
        for row in range(1, 4):
            result = result + dr[axis, row].astype(F32)
        out_ref[:, axis * HEAD : (axis + 1) * HEAD] = result * factor


def on_device(embeds, out_grad, w_query, w_key, w_value, lengths, item_rows, tile_owner):
    vmem = pl.BlockSpec(memory_space=pltpu.VMEM)
    smem = pl.BlockSpec(memory_space=pltpu.SMEM)
    copies = 3 + 6 + 14 + 28 + 3 + 6
    return pl.pallas_call(
        kernel,
        out_shape=jax.ShapeDtypeStruct((ROWS, 2 * HEAD), F32),
        in_specs=[smem, smem] + [vmem] * 6,
        out_specs=vmem,
        scratch_shapes=[
            pltpu.VMEM((16, TILE, 2 * HEAD), BF16),
            pltpu.SMEM((16,), jnp.int32),
            pltpu.VMEM((4, 8, TILE), jnp.int32),
            pltpu.VMEM((4, 8, TILE), jnp.int32),
            pltpu.VMEM((2, 4, 2 * TILE, 2 * HEAD), BF16),
            pltpu.VMEM((2, 4, 2 * TILE, 2 * HEAD), BF16),
            pltpu.VMEM((2, 8, 8, TILE), F32),
            pltpu.VMEM((2, 8, 8, TILE), F32),
            pltpu.VMEM((2, 2, 8, 4, 64, HEAD), BF16),
            pltpu.VMEM((2, 2, 8, 4, 64, HEAD), BF16),
            pltpu.VMEM((8, TILE), F32),
            pltpu.VMEM((4, 8, TILE), F32),
            pltpu.VMEM((2, 4, ROWS, HEAD), F32),
            pltpu.VMEM((2, 4, ROWS, HEAD), BF16),
            pltpu.VMEM((2, 4, ROWS, HEAD), BF16),
            pltpu.SemaphoreType.DMA((copies,)),
            pltpu.SemaphoreType.DMA((copies,)),
        ],
        compiler_params=pltpu.CompilerParams(
            collective_id=0, has_side_effects=True, vmem_limit_bytes=60 << 20
        ),
        name="gated_attention_table_grad",
    )(
        lengths,
        tile_owner,
        item_rows.reshape(-1, TILE),
        embeds,
        out_grad,
        w_query,
        w_key,
        w_value,
    )


def solution(mesh):
    both = ("group", "batch")
    placed = (P(both, None), P(both, None), P(), P(), P(), P(both), P(both), P(both))
    return jax.shard_map(
        on_device, mesh=mesh, in_specs=placed, out_specs=P(both, None), check_vma=False
    )
```

```python
import functools
import math

import jax
import jax.numpy as jnp
from jax import lax
from jax.experimental import pallas as pl
from jax.experimental.pallas import tpu as pltpu
from jax.sharding import PartitionSpec as P

SEQ = 512
TILE = 128
HEAD = 128
BLOCK = 128
ROWS = 256
MESH_ID = pl.DeviceIdType.MESH
F32 = jnp.float32
BF16 = jnp.bfloat16


def dot(a, b, dims):
    return lax.dot_general(a, b, ((dims[:1], dims[1:]), ((), ())), preferred_element_type=F32)


def iota(shape, dim):
    return lax.broadcasted_iota(jnp.int32, shape, dim)


def onehot(rows, index):
    return jnp.where(iota((rows, index.shape[1]), 0) == index, 1.0, 0.0).astype(BF16)


def gate(raw, attend_grad, weight):
    half = raw * (0.5 / math.sqrt(HEAD))
    tanh = jnp.tanh(half)
    gated = (1.0 + tanh) * weight
    attend = half * gated
    score = (attend_grad * gated) * (1.0 + half * (1.0 - tanh))
    return attend.astype(BF16), score.astype(BF16)


def history(item, len_ref, emb, grad, wq, wk, wv, tok_ref):
    span = pl.ds(item * SEQ, SEQ)
    embeds, grads = emb[span, :], grad[span, :]
    query = dot(embeds, wq[...], (1, 0)).astype(BF16)
    keys = dot(embeds, wk[...], (1, 0)).astype(BF16)
    value = dot(embeds, wv[...], (1, 0)).astype(BF16)
    counts = jnp.full((1, SEQ), len_ref[item], jnp.int32)
    weight = jnp.where(iota((1, SEQ), 1) < counts, 1.0 / counts.astype(F32), 0.0)
    causal = iota((BLOCK, BLOCK), 1) >= iota((BLOCK, BLOCK), 0)
    empty = jnp.zeros((BLOCK, BLOCK), BF16)
    wide = 2 * BLOCK
    parts = [[], [], []]
    for head in range(2):
        cols = slice(head * HEAD, (head + 1) * HEAD)
        totals = [[None, None], [None, None], [None, None]]

        def add(which, block, piece):
            old = totals[which][block]
            totals[which][block] = piece if old is None else old + piece

        for j, i in ((0, 1), (0, 0), (1, 1)):
            rows, others = slice(j * wide, (j + 1) * wide), slice(i * wide, (i + 1) * wide)
            k, v, q, g = keys[rows, cols], value[rows, cols], query[others, cols], grads[others, cols]
            raw = dot(k, q, (1, 1))
            attend_grad = dot(v, g, (1, 1))
            w = weight[:, others]
            if j == i:
                first = jnp.where(causal, w[:, :BLOCK], 0.0)
                last = jnp.where(causal, w[:, BLOCK:], 0.0)
                rest = jnp.broadcast_to(w[:, BLOCK:], (BLOCK, BLOCK))
                upper = gate(raw[:BLOCK], attend_grad[:BLOCK], jnp.concatenate([first, rest], axis=1))
                lower = gate(raw[BLOCK:, BLOCK:], attend_grad[BLOCK:, BLOCK:], last)
                attend, score = (
                    jnp.concatenate([a, jnp.concatenate([empty, b], axis=1)], axis=0)
                    for a, b in zip(upper, lower)
                )
            else:
                attend, score = gate(raw, attend_grad, w)
            add(2, j, dot(attend, g, (1, 0)))
            add(1, j, dot(score, q, (1, 0)))
            add(0, i, dot(score, k, (0, 0)))
        scales = (0.5 / math.sqrt(HEAD), 0.5 / math.sqrt(HEAD), None)
        for which in range(3):
            whole = jnp.concatenate(totals[which], axis=0)
            if scales[which] is not None:
                whole = whole * scales[which]
            parts[which].append(whole.astype(BF16))
    token = None
    for which, w in enumerate((wq, wk, wv)):
        piece = dot(jnp.concatenate(parts[which], axis=1), w[...], (1, 1))
        token = piece if token is None else token + piece
    tiles = SEQ // TILE
    tok_ref[pl.ds(item * tiles, tiles)] = token.astype(BF16).reshape(tiles, TILE, 2 * HEAD)


def kernel(
    len_ref, owner_ref, rows_hbm, emb_hbm, og_hbm, wq_hbm, wk_hbm, wv_hbm, out_ref,
    rows_ref, emb, grad, wq, wk, wv, in_sem,
    tok, order, m1s, m1r, zs, zr, m2s, m2r, ss, sr, m3s, m3r, hot, acc, ds_, dr,
    send_sem, m1_sem, z_sem, m2_sem, s_sem, m3_sem, d_sem,
):
    group = lax.axis_index("group")
    batch = lax.axis_index("batch")
    my_x, my_y, my_c = batch // 8, lax.rem(batch // 2, 4), lax.rem(batch, 2)

    def device(dx=0, dy=0, dz=0, dc=0):
        x, y = lax.rem(my_x + dx, 4), lax.rem(my_y + dy, 4)
        return (lax.rem(group + dz, 4), x * 8 + y * 2 + lax.rem(my_c + dc, 2))

    def line(axis, d):
        return device(dx=d // 2, dc=d % 2) if axis == 0 else device(dy=d // 2, dc=d % 2)

    peers = [device(dz=d) for d in (1, 2, 3)]
    peers += [line(0, d) for d in range(1, 8)] + [line(1, d) for d in range(2, 8)]
    barrier = pltpu.get_barrier_semaphore()
    for peer in peers:
        pl.semaphore_signal(barrier, inc=1, device_id=peer, device_id_type=MESH_ID)

    loads = [[] for _ in range(5)]

    def load(stage, source, target):
        copy = pltpu.make_async_copy(source, target, in_sem.at[stage])
        copy.start()
        loads[stage].append(copy)

    for source, target in ((wq_hbm, wq), (wk_hbm, wk), (wv_hbm, wv), (rows_hbm, rows_ref)):
        load(0, source, target)
    for item in range(4):
        span = pl.ds(item * SEQ, SEQ)
        load(item + 1 if item else 0, emb_hbm.at[span, :], emb.at[span, :])
        load(item + 1 if item else 0, og_hbm.at[span, :], grad.at[span, :])

    sent = []

    def remote(source, target, sem, peer):
        copy = pltpu.make_async_remote_copy(
            src_ref=source,
            dst_ref=target,
            send_sem=send_sem,
            recv_sem=sem,
            device_id=peer,
            device_id_type=MESH_ID,
        )
        copy.start()
        sent.append(copy)

    def arrived(target, sem):
        pltpu.make_async_copy(target, target, sem).wait()

    live = len_ref[0] + len_ref[1] + len_ref[2] + len_ref[3]
    for half in range(2):
        owner = [owner_ref[half * 8 + t] for t in range(8)]
        place = []
        for t in range(8):
            at = 2 * owner[t]
            for other in owner[:t]:
                at = at + jnp.where(other == owner[t], 1, 0)
            place.append(at)
        for p in range(8):
            tile = 0
            for t in range(1, 8):
                tile = tile + jnp.where(place[t] == p, t, 0)
            order[half * 8 + p] = tile + half * 8

    def owned(half, dz, k):
        return order[half * 8 + 2 * lax.rem(group + dz, 4) + k]

    def compute(item):
        for copy in loads[item + 1 if item else 0]:
            copy.wait()
        history(item, len_ref, emb, grad, wq, wk, wv, tok)

    compute(0)
    pl.semaphore_wait(barrier, len(peers))
    for dz in range(4):
        target = m1s.at[dz] if dz else m1r.at[0]
        for half in range(2):
            for k in range(2):
                target[half * 2 + k : half * 2 + k + 1, :] = rows_ref[pl.ds(owned(half, dz, k), 1), :]
        target[4:5, :] = jnp.full((1, TILE), live, jnp.int32)
        target[5:8, :] = jnp.zeros((3, TILE), jnp.int32)
    for dz in range(1, 4):
        remote(m1s.at[dz], m1r.at[dz], m1_sem, device(dz=dz))

    def send_tiles(half):
        for dz in (1, 3, 2):
            for k in range(2):
                zs[half, dz, pl.ds(k * TILE, TILE), :] = tok[owned(half, dz, k)]
            remote(zs.at[half, dz], zr.at[half, dz], z_sem.at[half * 4 + dz], device(dz=dz))
        for k in range(2):
            zr[half, 0, pl.ds(k * TILE, TILE), :] = tok[owned(half, 0, k)]

    compute(1)
    send_tiles(0)

    arrived(m1r.at[1:4], m1_sem)
    heads = jnp.concatenate(
        [m1r[dz, half * 2 + k : half * 2 + k + 1, :] for half in range(2) for dz in range(4) for k in range(2)],
        axis=0,
    )
    holder = heads // ROWS
    local = lax.rem(heads, ROWS)
    before = jnp.where(iota((TILE, TILE), 0) < iota((TILE, TILE), 1), 1.0, 0.0).astype(BF16)
    marks = jnp.concatenate([onehot(32, holder[u : u + 1, :]) for u in range(16)], axis=0)
    earlier = dot(marks, before, (1, 0)) * marks.astype(F32)
    rank = jnp.concatenate(
        [jnp.sum(earlier[u * 32 : (u + 1) * 32], axis=0, keepdims=True) for u in range(16)], axis=0
    ).astype(jnp.int32)
    away_x = lax.rem(holder // 8 + 4 - my_x, 4)
    away_y = lax.rem(lax.rem(holder // 2, 4) + 4 - my_y, 4)
    away_c = lax.rem(lax.rem(holder, 2) + 2 - my_c, 2)
    within = rank + 8 * lax.rem(iota((16, TILE), 0), 2)
    dest = [away_x * 2 + away_c, away_y * 2 + away_c]
    line_row = [away_y, away_x]
    slots = [dest[axis] * 64 + line_row[axis] * 16 + within for axis in range(2)]
    meta_row = [dest[axis] * 8 + line_row[axis] for axis in range(2)]
    meta_lane = within + 16 * (iota((16, TILE), 0) // 2)

    def pair(array, unit):
        return jnp.concatenate([array[2 * unit : 2 * unit + 1, :], array[2 * unit + 1 : 2 * unit + 2, :]], axis=1)

    live_z = m1r[0, 4:5, :] + m1r[1, 4:5, :] + m1r[2, 4:5, :] + m1r[3, 4:5, :]
    live_row = jnp.where(lax.rem(iota((64, TILE), 0), 8) == 4, live_z.astype(F32), 0.0)
    for axis in range(2):
        meta = live_row
        for unit in range(8):
            left = jnp.where(iota((64, 256), 0) == pair(meta_row[axis], unit), pair(local, unit).astype(F32), 0.0)
            meta = meta + dot(left.astype(BF16), onehot(TILE, pair(meta_lane, unit)), (1, 1))
        for d in range(8):
            target = m2s.at[axis, d] if d else m2r.at[axis, 0]
            target[...] = meta[d * 8 : (d + 1) * 8, :]
        for d in range(1, 8):
            remote(m2s.at[axis, d], m2r.at[axis, d], m2_sem, line(axis, d))


    def forward(half, dz):
        for axis in range(2):
            packed = dot(
                onehot(512, pair(slots[axis], half * 4 + dz)),
                zr[half, dz, :, axis * HEAD : (axis + 1) * HEAD],
                (1, 0),
            ).astype(BF16)
            for d in range(8):
                target = ss.at[half, axis, d, dz] if d else sr.at[half, axis, 0, dz]
                for row in range(4):
                    target[row] = packed[d * 64 + row * 16 : d * 64 + row * 16 + 16]
        for d in (4, 5, 2, 6, 3, 7, 1):
            for axis in range(2):
                remote(ss.at[half, axis, d, dz], sr.at[half, axis, d, dz], s_sem.at[half * 4 + dz], line(axis, d))

    def relay(half, dz):
        arrived(zr.at[half, dz], z_sem.at[half * 4 + dz])
        forward(half, dz)

    forward(0, 0)
    compute(2)
    relay(0, 1)
    compute(3)
    send_tiles(1)
    relay(0, 3)
    forward(1, 0)
    relay(0, 2)

    arrived(m2r.at[:, 1:8], m2_sem)
    live_x = m2r[0, 0, 4:5, :]
    for d in range(1, 8):
        live_x = live_x + m2r[0, d, 4:5, :]
    live_x = jnp.broadcast_to(live_x, (8, TILE))
    m3r[0] = live_x
    m3s[...] = live_x
    for dy in (1, 2, 3):
        remote(m3s, m3r.at[dy], m3_sem, device(dy=dy))

    low = iota((8, TILE), 1) < 64
    for half in range(2):
        for axis in range(2):
            index = []
            for d in range(0, 8, 2):
                a, b = m2r[axis, d], m2r[axis, d + 1]
                if half == 0:
                    index.append(jnp.where(low, a, pltpu.roll(b, 64, 1)))
                else:
                    index.append(jnp.where(low, pltpu.roll(a, 64, 1), b))
            index = jnp.concatenate(index, axis=1).astype(jnp.int32)
            for row in range(4):
                hot[half, axis, row] = onehot(ROWS, index[row : row + 1, :])

    for dz in (1, 3, 2):
        relay(1, dz)

    for half in range(2):
        for dz in ((0, 1, 3, 2) if half == 0 else (0, 1, 3, 2)):
            arrived(sr.at[half, :, 1:8, dz], s_sem.at[half * 4 + dz])
        for row in (1, 2, 3, 0):
            for axis in range(2):
                data = sr[half, axis, :, :, row].reshape(512, HEAD)
                part = dot(hot[half, axis, row], data, (1, 0))
                if half == 0:
                    acc[axis, row] = part
                elif row == 0:
                    acc[axis, 0] = acc[axis, 0] + part
                else:
                    ds_[axis, row] = (acc[axis, row] + part).astype(BF16)
                    peer = device(dy=row) if axis == 0 else device(dx=row)
                    remote(ds_.at[axis, row], dr.at[axis, row], d_sem, peer)

    arrived(m3r.at[1:4], m3_sem)
    total_live = m3r[0] + m3r[1] + m3r[2] + m3r[3]
    factor = (float(SEQ * 4 * 128) / total_live)[:1]
    arrived(dr.at[:, 1:4], d_sem)
    for axis in range(2):
        result = acc[axis, 0]
        for row in range(1, 4):
            result = result + dr[axis, row].astype(F32)
        out_ref[:, axis * HEAD : (axis + 1) * HEAD] = result * factor
    for copy in sent:
        copy.wait_send()


def on_device(embeds, out_grad, w_query, w_key, w_value, lengths, item_rows, tile_owner):
    vmem = pl.BlockSpec(memory_space=pltpu.VMEM)
    smem = pl.BlockSpec(memory_space=pltpu.SMEM)
    width = 2 * HEAD
    total = pl.pallas_call(
        kernel,
        out_shape=jax.ShapeDtypeStruct((ROWS, width), F32),
        in_specs=[smem, smem] + [pl.BlockSpec(memory_space=pl.ANY)] * 6,
        out_specs=vmem,
        scratch_shapes=[
            pltpu.VMEM((16, TILE), jnp.int32),
            pltpu.VMEM((4 * SEQ, width), BF16),
            pltpu.VMEM((4 * SEQ, width), BF16),
            pltpu.VMEM((width, width), BF16),
            pltpu.VMEM((width, width), BF16),
            pltpu.VMEM((width, width), BF16),
            pltpu.SemaphoreType.DMA((5,)),
            pltpu.VMEM((16, TILE, 2 * HEAD), BF16),
            pltpu.SMEM((16,), jnp.int32),
            pltpu.VMEM((4, 8, TILE), jnp.int32),
            pltpu.VMEM((4, 8, TILE), jnp.int32),
            pltpu.VMEM((2, 4, 2 * TILE, 2 * HEAD), BF16),
            pltpu.VMEM((2, 4, 2 * TILE, 2 * HEAD), BF16),
            pltpu.VMEM((2, 8, 8, TILE), F32),
            pltpu.VMEM((2, 8, 8, TILE), F32),
            pltpu.VMEM((2, 2, 8, 4, 4, 16, HEAD), BF16),
            pltpu.VMEM((2, 2, 8, 4, 4, 16, HEAD), BF16),
            pltpu.VMEM((8, TILE), F32),
            pltpu.VMEM((4, 8, TILE), F32),
            pltpu.VMEM((2, 2, 4, ROWS, 512), BF16),
            pltpu.VMEM((2, 4, ROWS, HEAD), F32),
            pltpu.VMEM((2, 4, ROWS, HEAD), BF16),
            pltpu.VMEM((2, 4, ROWS, HEAD), BF16),
            pltpu.SemaphoreType.DMA(()),
            pltpu.SemaphoreType.DMA(()),
            pltpu.SemaphoreType.DMA((8,)),
            pltpu.SemaphoreType.DMA(()),
            pltpu.SemaphoreType.DMA((8,)),
            pltpu.SemaphoreType.DMA(()),
            pltpu.SemaphoreType.DMA(()),
        ],
        compiler_params=pltpu.CompilerParams(
            collective_id=0, has_side_effects=True, vmem_limit_bytes=60 << 20
        ),
        name="gated_attention_table_grad",
    )(
        lengths,
        tile_owner,
        item_rows.reshape(-1, TILE),
        embeds,
        out_grad,
        w_query,
        w_key,
        w_value,
    )
    return total


def solution(mesh):
    both = ("group", "batch")
    placed = (P(both, None), P(both, None), P(), P(), P(), P(both), P(both), P(both))
    return jax.shard_map(
        on_device, mesh=mesh, in_specs=placed, out_specs=P(both, None), check_vma=False
    )
```

```python
import functools
import math

import jax
import jax.numpy as jnp
from jax import lax
from jax.experimental import pallas as pl
from jax.experimental.pallas import tpu as pltpu
from jax.sharding import PartitionSpec as P

SEQ = 512
TILE = 128
HEAD = 128
BLOCK = 128
ROWS = 256
MESH_ID = pl.DeviceIdType.MESH
F32 = jnp.float32
BF16 = jnp.bfloat16


def dot(a, b, dims):
    return lax.dot_general(a, b, ((dims[:1], dims[1:]), ((), ())), preferred_element_type=F32)


def iota(shape, dim):
    return lax.broadcasted_iota(jnp.int32, shape, dim)


def onehot(rows, index):
    return jnp.where(iota((rows, index.shape[1]), 0) == index, 1.0, 0.0).astype(BF16)


def gate(raw, attend_grad, weight):
    half = raw * (0.5 / math.sqrt(HEAD))
    tanh = jnp.tanh(half)
    gated = (1.0 + tanh) * weight
    attend = half * gated
    score = (attend_grad * gated) * (1.0 + half * (1.0 - tanh))
    return attend.astype(BF16), score.astype(BF16)


def history(item, len_ref, emb, grad, wq, wk, wv, tok_ref):
    span = pl.ds(item * SEQ, SEQ)
    embeds, grads = emb[span, :], grad[span, :]
    query = dot(embeds, wq[...], (1, 0)).astype(BF16)
    keys = dot(embeds, wk[...], (1, 0)).astype(BF16)
    value = dot(embeds, wv[...], (1, 0)).astype(BF16)
    counts = jnp.full((1, SEQ), len_ref[item], jnp.int32)
    weight = jnp.where(iota((1, SEQ), 1) < counts, 1.0 / counts.astype(F32), 0.0)
    causal = iota((BLOCK, BLOCK), 1) >= iota((BLOCK, BLOCK), 0)
    empty = jnp.zeros((BLOCK, BLOCK), BF16)
    wide = 2 * BLOCK
    parts = [[], [], []]
    for head in range(2):
        cols = slice(head * HEAD, (head + 1) * HEAD)
        totals = [[None, None], [None, None], [None, None]]

        def add(which, block, piece):
            old = totals[which][block]
            totals[which][block] = piece if old is None else old + piece

        for j, i in ((0, 1), (0, 0), (1, 1)):
            rows, others = slice(j * wide, (j + 1) * wide), slice(i * wide, (i + 1) * wide)
            k, v, q, g = keys[rows, cols], value[rows, cols], query[others, cols], grads[others, cols]
            raw = dot(k, q, (1, 1))
            attend_grad = dot(v, g, (1, 1))
            w = weight[:, others]
            if j == i:
                first = jnp.where(causal, w[:, :BLOCK], 0.0)
                last = jnp.where(causal, w[:, BLOCK:], 0.0)
                rest = jnp.broadcast_to(w[:, BLOCK:], (BLOCK, BLOCK))
                upper = gate(raw[:BLOCK], attend_grad[:BLOCK], jnp.concatenate([first, rest], axis=1))
                lower = gate(raw[BLOCK:, BLOCK:], attend_grad[BLOCK:, BLOCK:], last)
                attend, score = (
                    jnp.concatenate([a, jnp.concatenate([empty, b], axis=1)], axis=0)
                    for a, b in zip(upper, lower)
                )
            else:
                attend, score = gate(raw, attend_grad, w)
            add(2, j, dot(attend, g, (1, 0)))
            add(1, j, dot(score, q, (1, 0)))
            add(0, i, dot(score, k, (0, 0)))
        scales = (0.5 / math.sqrt(HEAD), 0.5 / math.sqrt(HEAD), None)
        for which in range(3):
            whole = jnp.concatenate(totals[which], axis=0)
            if scales[which] is not None:
                whole = whole * scales[which]
            parts[which].append(whole.astype(BF16))
    token = None
    for which, w in enumerate((wq, wk, wv)):
        piece = dot(jnp.concatenate(parts[which], axis=1), w[...], (1, 1))
        token = piece if token is None else token + piece
    tiles = SEQ // TILE
    tok_ref[pl.ds(item * tiles, tiles)] = token.astype(BF16).reshape(tiles, TILE, 2 * HEAD)


def kernel(
    len_ref, owner_ref, rows_hbm, emb_hbm, og_hbm, wq_hbm, wk_hbm, wv_hbm, out_ref,
    rows_ref, emb, grad, wq, wk, wv, in_sem,
    tok, order, m1s, m1r, zs, zr, m2s, m2r, ss, sr, m3s, m3r, hot, acc, ds_, dr,
    send_sem, m1_sem, z_sem, m2_sem, s_sem, m3_sem, d_sem,
):
    group = lax.axis_index("group")
    batch = lax.axis_index("batch")
    my_x, my_y, my_c = batch // 8, lax.rem(batch // 2, 4), lax.rem(batch, 2)

    def device(dx=0, dy=0, dz=0, dc=0):
        x, y = lax.rem(my_x + dx, 4), lax.rem(my_y + dy, 4)
        return (lax.rem(group + dz, 4), x * 8 + y * 2 + lax.rem(my_c + dc, 2))

    def line(axis, d):
        return device(dx=d // 2, dc=d % 2) if axis == 0 else device(dy=d // 2, dc=d % 2)

    peers = [device(dz=d) for d in (1, 2, 3)]
    peers += [line(0, d) for d in range(1, 8)] + [line(1, d) for d in range(2, 8)]
    barrier = pltpu.get_barrier_semaphore()
    for peer in peers:
        pl.semaphore_signal(barrier, inc=1, device_id=peer, device_id_type=MESH_ID)

    loads = [[] for _ in range(5)]

    def load(stage, source, target):
        copy = pltpu.make_async_copy(source, target, in_sem.at[stage])
        copy.start()
        loads[stage].append(copy)

    for source, target in ((wq_hbm, wq), (wk_hbm, wk), (wv_hbm, wv), (rows_hbm, rows_ref)):
        load(0, source, target)
    for item in range(4):
        span = pl.ds(item * SEQ, SEQ)
        load(item + 1 if item else 0, emb_hbm.at[span, :], emb.at[span, :])
        load(item + 1 if item else 0, og_hbm.at[span, :], grad.at[span, :])

    sent = []

    def remote(source, target, sem, peer):
        copy = pltpu.make_async_remote_copy(
            src_ref=source,
            dst_ref=target,
            send_sem=send_sem,
            recv_sem=sem,
            device_id=peer,
            device_id_type=MESH_ID,
        )
        copy.start()
        sent.append(copy)

    def arrived(target, sem):
        pltpu.make_async_copy(target, target, sem).wait()

    live = len_ref[0] + len_ref[1] + len_ref[2] + len_ref[3]
    for half in range(2):
        owner = [owner_ref[half * 8 + t] for t in range(8)]
        place = []
        for t in range(8):
            at = 2 * owner[t]
            for other in owner[:t]:
                at = at + jnp.where(other == owner[t], 1, 0)
            place.append(at)
        for p in range(8):
            tile = 0
            for t in range(1, 8):
                tile = tile + jnp.where(place[t] == p, t, 0)
            order[half * 8 + p] = tile + half * 8

    def owned(half, dz, k):
        return order[half * 8 + 2 * lax.rem(group + dz, 4) + k]

    def compute(item):
        for copy in loads[item + 1 if item else 0]:
            copy.wait()
        history(item, len_ref, emb, grad, wq, wk, wv, tok)

    compute(0)
    pl.semaphore_wait(barrier, len(peers))
    for dz in range(4):
        target = m1s.at[dz] if dz else m1r.at[0]
        for half in range(2):
            for k in range(2):
                target[half * 2 + k : half * 2 + k + 1, :] = rows_ref[pl.ds(owned(half, dz, k), 1), :]
        target[4:5, :] = jnp.full((1, TILE), live, jnp.int32)
        target[5:8, :] = jnp.zeros((3, TILE), jnp.int32)
    for dz in range(1, 4):
        remote(m1s.at[dz], m1r.at[dz], m1_sem, device(dz=dz))

    def send_tiles(half):
        for dz in (1, 3, 2):
            for k in range(2):
                zs[half, dz, pl.ds(k * TILE, TILE), :] = tok[owned(half, dz, k)]
            remote(zs.at[half, dz], zr.at[half, dz], z_sem.at[half * 4 + dz], device(dz=dz))
        for k in range(2):
            zr[half, 0, pl.ds(k * TILE, TILE), :] = tok[owned(half, 0, k)]

    compute(1)
    send_tiles(0)

    def forward(half, dz):
        for axis in range(2):
            packed = dot(
                onehot(512, pair(slots[axis], half * 4 + dz)),
                zr[half, dz, :, axis * HEAD : (axis + 1) * HEAD],
                (1, 0),
            ).astype(BF16)
            for d in range(8):
                target = ss.at[half, axis, d, dz] if d else sr.at[half, axis, 0, dz]
                for row in range(4):
                    target[row] = packed[d * 64 + row * 16 : d * 64 + row * 16 + 16]
        for d in (4, 5, 2, 6, 3, 7, 1):
            for axis in range(2):
                remote(ss.at[half, axis, d, dz], sr.at[half, axis, d, dz], s_sem.at[half * 4 + dz], line(axis, d))

    def relay(half, dz):
        arrived(zr.at[half, dz], z_sem.at[half * 4 + dz])
        forward(half, dz)

    compute(2)

    arrived(m1r.at[1:4], m1_sem)
    heads = jnp.concatenate(
        [m1r[dz, half * 2 + k : half * 2 + k + 1, :] for half in range(2) for dz in range(4) for k in range(2)],
        axis=0,
    )
    holder = heads // ROWS
    local = lax.rem(heads, ROWS)
    before = jnp.where(iota((TILE, TILE), 0) < iota((TILE, TILE), 1), 1.0, 0.0).astype(BF16)
    marks = jnp.concatenate([onehot(32, holder[u : u + 1, :]) for u in range(16)], axis=0)
    earlier = dot(marks, before, (1, 0)) * marks.astype(F32)
    rank = jnp.concatenate(
        [jnp.sum(earlier[u * 32 : (u + 1) * 32], axis=0, keepdims=True) for u in range(16)], axis=0
    ).astype(jnp.int32)
    away_x = lax.rem(holder // 8 + 4 - my_x, 4)
    away_y = lax.rem(lax.rem(holder // 2, 4) + 4 - my_y, 4)
    away_c = lax.rem(lax.rem(holder, 2) + 2 - my_c, 2)
    within = rank + 8 * lax.rem(iota((16, TILE), 0), 2)
    dest = [away_x * 2 + away_c, away_y * 2 + away_c]
    line_row = [away_y, away_x]
    slots = [dest[axis] * 64 + line_row[axis] * 16 + within for axis in range(2)]
    meta_row = [dest[axis] * 8 + line_row[axis] for axis in range(2)]
    meta_lane = within + 16 * (iota((16, TILE), 0) // 2)

    def pair(array, unit):
        return jnp.concatenate([array[2 * unit : 2 * unit + 1, :], array[2 * unit + 1 : 2 * unit + 2, :]], axis=1)

    live_z = m1r[0, 4:5, :] + m1r[1, 4:5, :] + m1r[2, 4:5, :] + m1r[3, 4:5, :]
    live_row = jnp.where(lax.rem(iota((64, TILE), 0), 8) == 4, live_z.astype(F32), 0.0)
    for axis in range(2):
        meta = live_row
        for unit in range(8):
            left = jnp.where(iota((64, 256), 0) == pair(meta_row[axis], unit), pair(local, unit).astype(F32), 0.0)
            meta = meta + dot(left.astype(BF16), onehot(TILE, pair(meta_lane, unit)), (1, 1))
        for d in range(8):
            target = m2s.at[axis, d] if d else m2r.at[axis, 0]
            target[...] = meta[d * 8 : (d + 1) * 8, :]
        for d in range(1, 8):
            remote(m2s.at[axis, d], m2r.at[axis, d], m2_sem, line(axis, d))


    forward(0, 0)
    compute(3)
    send_tiles(1)
    relay(0, 1)
    relay(0, 3)
    forward(1, 0)
    relay(0, 2)

    arrived(m2r.at[:, 1:8], m2_sem)
    live_x = m2r[0, 0, 4:5, :]
    for d in range(1, 8):
        live_x = live_x + m2r[0, d, 4:5, :]
    live_x = jnp.broadcast_to(live_x, (8, TILE))
    m3r[0] = live_x
    m3s[...] = live_x
    for dy in (1, 2, 3):
        remote(m3s, m3r.at[dy], m3_sem, device(dy=dy))

    low = iota((8, TILE), 1) < 64
    for half in range(2):
        for axis in range(2):
            index = []
            for d in range(0, 8, 2):
                a, b = m2r[axis, d], m2r[axis, d + 1]
                if half == 0:
                    index.append(jnp.where(low, a, pltpu.roll(b, 64, 1)))
                else:
                    index.append(jnp.where(low, pltpu.roll(a, 64, 1), b))
            index = jnp.concatenate(index, axis=1).astype(jnp.int32)
            for row in range(4):
                hot[half, axis, row] = onehot(ROWS, index[row : row + 1, :])

    for dz in (1, 3, 2):
        relay(1, dz)

    for half in range(2):
        for dz in ((0, 1, 3, 2) if half == 0 else (0, 1, 3, 2)):
            arrived(sr.at[half, :, 1:8, dz], s_sem.at[half * 4 + dz])
        for row in (1, 2, 3, 0):
            for axis in range(2):
                data = sr[half, axis, :, :, row].reshape(512, HEAD)
                part = dot(hot[half, axis, row], data, (1, 0))
                if half == 0:
                    acc[axis, row] = part
                elif row == 0:
                    acc[axis, 0] = acc[axis, 0] + part
                else:
                    ds_[axis, row] = (acc[axis, row] + part).astype(BF16)
            if half == 1 and row == 3:
                for away in (2, 1, 3):
                    remote(ds_.at[0, away], dr.at[0, away], d_sem, device(dy=away))
                    remote(ds_.at[1, away], dr.at[1, away], d_sem, device(dx=away))

    arrived(m3r.at[1:4], m3_sem)
    total_live = m3r[0] + m3r[1] + m3r[2] + m3r[3]
    factor = (float(SEQ * 4 * 128) / total_live)[:1]
    arrived(dr.at[:, 1:4], d_sem)
    for axis in range(2):
        result = acc[axis, 0]
        for row in range(1, 4):
            result = result + dr[axis, row].astype(F32)
        out_ref[:, axis * HEAD : (axis + 1) * HEAD] = result * factor
    for copy in sent:
        copy.wait_send()


def on_device(embeds, out_grad, w_query, w_key, w_value, lengths, item_rows, tile_owner):
    vmem = pl.BlockSpec(memory_space=pltpu.VMEM)
    smem = pl.BlockSpec(memory_space=pltpu.SMEM)
    width = 2 * HEAD
    total = pl.pallas_call(
        kernel,
        out_shape=pltpu.VMEM((ROWS, width), F32),
        in_specs=[smem, smem] + [pl.BlockSpec(memory_space=pl.ANY)] * 6,
        out_specs=vmem,
        scratch_shapes=[
            pltpu.VMEM((16, TILE), jnp.int32),
            pltpu.VMEM((4 * SEQ, width), BF16),
            pltpu.VMEM((4 * SEQ, width), BF16),
            pltpu.VMEM((width, width), BF16),
            pltpu.VMEM((width, width), BF16),
            pltpu.VMEM((width, width), BF16),
            pltpu.SemaphoreType.DMA((5,)),
            pltpu.VMEM((16, TILE, 2 * HEAD), BF16),
            pltpu.SMEM((16,), jnp.int32),
            pltpu.VMEM((4, 8, TILE), jnp.int32),
            pltpu.VMEM((4, 8, TILE), jnp.int32),
            pltpu.VMEM((2, 4, 2 * TILE, 2 * HEAD), BF16),
            pltpu.VMEM((2, 4, 2 * TILE, 2 * HEAD), BF16),
            pltpu.VMEM((2, 8, 8, TILE), F32),
            pltpu.VMEM((2, 8, 8, TILE), F32),
            pltpu.VMEM((2, 2, 8, 4, 4, 16, HEAD), BF16),
            pltpu.VMEM((2, 2, 8, 4, 4, 16, HEAD), BF16),
            pltpu.VMEM((8, TILE), F32),
            pltpu.VMEM((4, 8, TILE), F32),
            pltpu.VMEM((2, 2, 4, ROWS, 512), BF16),
            pltpu.VMEM((2, 4, ROWS, HEAD), F32),
            pltpu.VMEM((2, 4, ROWS, HEAD), BF16),
            pltpu.VMEM((2, 4, ROWS, HEAD), BF16),
            pltpu.SemaphoreType.DMA(()),
            pltpu.SemaphoreType.DMA(()),
            pltpu.SemaphoreType.DMA((8,)),
            pltpu.SemaphoreType.DMA(()),
            pltpu.SemaphoreType.DMA((8,)),
            pltpu.SemaphoreType.DMA(()),
            pltpu.SemaphoreType.DMA(()),
        ],
        compiler_params=pltpu.CompilerParams(
            collective_id=0, has_side_effects=True, vmem_limit_bytes=60 << 20
        ),
        name="gated_attention_table_grad",
    )(
        lengths,
        tile_owner,
        item_rows.reshape(-1, TILE),
        embeds,
        out_grad,
        w_query,
        w_key,
        w_value,
    )
    return total


def solution(mesh):
    both = ("group", "batch")
    placed = (P(both, None), P(both, None), P(), P(), P(), P(both), P(both), P(both))
    return jax.shard_map(
        on_device, mesh=mesh, in_specs=placed, out_specs=P(both, None), check_vma=False
    )
```

```python
import functools
import math

import jax
import jax.numpy as jnp
from jax import lax
from jax.experimental import pallas as pl
from jax.experimental.pallas import tpu as pltpu
from jax.sharding import PartitionSpec as P

SEQ = 512
TILE = 128
HEAD = 128
BLOCK = 128
ROWS = 256
MESH_ID = pl.DeviceIdType.MESH
F32 = jnp.float32
BF16 = jnp.bfloat16


def dot(a, b, dims):
    return lax.dot_general(a, b, ((dims[:1], dims[1:]), ((), ())), preferred_element_type=F32)


def iota(shape, dim):
    return lax.broadcasted_iota(jnp.int32, shape, dim)


def onehot(rows, index):
    return jnp.where(iota((rows, index.shape[1]), 0) == index, 1.0, 0.0).astype(BF16)


def gate(raw, attend_grad, weight):
    half = raw * (0.5 / math.sqrt(HEAD))
    tanh = jnp.tanh(half)
    gated = (1.0 + tanh) * weight
    attend = half * gated
    score = (attend_grad * gated) * (1.0 + half * (1.0 - tanh))
    return attend.astype(BF16), score.astype(BF16)


def history(item, len_ref, emb, grad, wq, wk, wv, tok_ref):
    span = pl.ds(item * SEQ, SEQ)
    embeds, grads = emb[span, :], grad[span, :]
    query = dot(embeds, wq[...], (1, 0)).astype(BF16)
    keys = dot(embeds, wk[...], (1, 0)).astype(BF16)
    value = dot(embeds, wv[...], (1, 0)).astype(BF16)
    counts = jnp.full((1, SEQ), len_ref[item], jnp.int32)
    weight = jnp.where(iota((1, SEQ), 1) < counts, 1.0 / counts.astype(F32), 0.0)
    causal = iota((BLOCK, BLOCK), 1) >= iota((BLOCK, BLOCK), 0)
    empty = jnp.zeros((BLOCK, BLOCK), BF16)
    wide = 2 * BLOCK
    parts = [[], [], []]
    for head in range(2):
        cols = slice(head * HEAD, (head + 1) * HEAD)
        totals = [[None, None], [None, None], [None, None]]

        def add(which, block, piece):
            old = totals[which][block]
            totals[which][block] = piece if old is None else old + piece

        for j, i in ((0, 1), (0, 0), (1, 1)):
            rows, others = slice(j * wide, (j + 1) * wide), slice(i * wide, (i + 1) * wide)
            k, v, q, g = keys[rows, cols], value[rows, cols], query[others, cols], grads[others, cols]
            raw = dot(k, q, (1, 1))
            attend_grad = dot(v, g, (1, 1))
            w = weight[:, others]
            if j == i:
                first = jnp.where(causal, w[:, :BLOCK], 0.0)
                last = jnp.where(causal, w[:, BLOCK:], 0.0)
                rest = jnp.broadcast_to(w[:, BLOCK:], (BLOCK, BLOCK))
                upper = gate(raw[:BLOCK], attend_grad[:BLOCK], jnp.concatenate([first, rest], axis=1))
                lower = gate(raw[BLOCK:, BLOCK:], attend_grad[BLOCK:, BLOCK:], last)
                attend, score = (
                    jnp.concatenate([a, jnp.concatenate([empty, b], axis=1)], axis=0)
                    for a, b in zip(upper, lower)
                )
            else:
                attend, score = gate(raw, attend_grad, w)
            add(2, j, dot(attend, g, (1, 0)))
            add(1, j, dot(score, q, (1, 0)))
            add(0, i, dot(score, k, (0, 0)))
        scales = (0.5 / math.sqrt(HEAD), 0.5 / math.sqrt(HEAD), None)
        for which in range(3):
            whole = jnp.concatenate(totals[which], axis=0)
            if scales[which] is not None:
                whole = whole * scales[which]
            parts[which].append(whole.astype(BF16))
    token = None
    for which, w in enumerate((wq, wk, wv)):
        piece = dot(jnp.concatenate(parts[which], axis=1), w[...], (1, 1))
        token = piece if token is None else token + piece
    tiles = SEQ // TILE
    tok_ref[pl.ds(item * tiles, tiles)] = token.astype(BF16).reshape(tiles, TILE, 2 * HEAD)


def kernel(
    len_ref, owner_ref, rows_hbm, emb_hbm, og_hbm, wq_hbm, wk_hbm, wv_hbm, out_ref,
    rows_ref, emb, grad, wq, wk, wv, in_sem,
    tok, order, m1s, m1r, zs, zr, m2s, m2r, ss, sr, m3s, m3r, hot, acc, ds_, dr,
    send_sem, near_sem, m1_sem, z_sem, m2_sem, s_sem, m3_sem, d_sem,
):
    group = lax.axis_index("group")
    batch = lax.axis_index("batch")
    my_x, my_y, my_c = batch // 8, lax.rem(batch // 2, 4), lax.rem(batch, 2)

    def device(dx=0, dy=0, dz=0, dc=0):
        x, y = lax.rem(my_x + dx, 4), lax.rem(my_y + dy, 4)
        return (lax.rem(group + dz, 4), x * 8 + y * 2 + lax.rem(my_c + dc, 2))

    def line(axis, d):
        return device(dx=d // 2, dc=d % 2) if axis == 0 else device(dy=d // 2, dc=d % 2)

    loads = [[] for _ in range(5)]

    def load(stage, source, target):
        copy = pltpu.make_async_copy(source, target, in_sem.at[stage])
        copy.start()
        loads[stage].append(copy)

    for source, target in ((wq_hbm, wq), (wk_hbm, wk), (wv_hbm, wv), (rows_hbm, rows_ref)):
        load(0, source, target)
    for item in range(4):
        span = pl.ds(item * SEQ, SEQ)
        load(item + 1 if item else 0, emb_hbm.at[span, :], emb.at[span, :])
        load(item + 1 if item else 0, og_hbm.at[span, :], grad.at[span, :])

    peers = [device(dz=d) for d in (1, 2, 3)]
    peers += [line(0, d) for d in range(1, 8)] + [line(1, d) for d in range(2, 8)]
    barrier = pltpu.get_barrier_semaphore()
    for peer in peers:
        pl.semaphore_signal(barrier, inc=1, device_id=peer, device_id_type=MESH_ID)

    sent = []

    def remote(source, target, sem, peer, left=None):
        copy = pltpu.make_async_remote_copy(
            src_ref=source,
            dst_ref=target,
            send_sem=send_sem if left is None else left,
            recv_sem=sem,
            device_id=peer,
            device_id_type=MESH_ID,
        )
        copy.start()
        if left is None:
            sent.append(copy)
        return copy

    def arrived(target, sem):
        pltpu.make_async_copy(target, target, sem).wait()

    live = len_ref[0] + len_ref[1] + len_ref[2] + len_ref[3]
    for half in range(2):
        owner = [owner_ref[half * 8 + t] for t in range(8)]
        place = []
        for t in range(8):
            at = 2 * owner[t]
            for other in owner[:t]:
                at = at + jnp.where(other == owner[t], 1, 0)
            place.append(at)
        for p in range(8):
            tile = 0
            for t in range(1, 8):
                tile = tile + jnp.where(place[t] == p, t, 0)
            order[half * 8 + p] = tile + half * 8

    def owned(half, dz, k):
        return order[half * 8 + 2 * lax.rem(group + dz, 4) + k]

    def compute(item):
        for copy in loads[item + 1 if item else 0]:
            copy.wait()
        history(item, len_ref, emb, grad, wq, wk, wv, tok)

    compute(0)
    pl.semaphore_wait(barrier, len(peers))
    for dz in range(4):
        target = m1s.at[dz] if dz else m1r.at[0]
        for half in range(2):
            for k in range(2):
                target[half * 2 + k : half * 2 + k + 1, :] = rows_ref[pl.ds(owned(half, dz, k), 1), :]
        target[4:5, :] = jnp.full((1, TILE), live, jnp.int32)
        target[5:8, :] = jnp.zeros((3, TILE), jnp.int32)
    for dz in range(1, 4):
        remote(m1s.at[dz], m1r.at[dz], m1_sem, device(dz=dz))

    def send_tiles(half):
        near = []
        for dz in (1, 3, 2):
            for k in range(2):
                zs[half, dz, pl.ds(k * TILE, TILE), :] = tok[owned(half, dz, k)]
            if dz != 2:
                left = near_sem.at[half]
                near.append(
                    remote(zs.at[half, dz], zr.at[half, dz], z_sem.at[half * 4 + dz], device(dz=dz), left)
                )
        for k in range(2):
            zr[half, 0, pl.ds(k * TILE, TILE), :] = tok[owned(half, 0, k)]
        return near

    def send_far(half, near):
        for copy in near:
            copy.wait_send()
        remote(zs.at[half, 2], zr.at[half, 2], z_sem.at[half * 4 + 2], device(dz=2))

    compute(1)
    near = send_tiles(0)

    def forward(half, dz):
        for axis in range(2):
            packed = dot(
                onehot(512, pair(slots[axis], half * 4 + dz)),
                zr[half, dz, :, axis * HEAD : (axis + 1) * HEAD],
                (1, 0),
            ).astype(BF16)
            for d in range(8):
                target = ss.at[half, axis, d, dz] if d else sr.at[half, axis, 0, dz]
                for row in range(4):
                    target[row] = packed[d * 64 + row * 16 : d * 64 + row * 16 + 16]
        for d in (4, 5, 2, 6, 3, 7, 1):
            for axis in range(2):
                remote(ss.at[half, axis, d, dz], sr.at[half, axis, d, dz], s_sem.at[half * 4 + dz], line(axis, d))

    def relay(half, dz):
        arrived(zr.at[half, dz], z_sem.at[half * 4 + dz])
        forward(half, dz)

    compute(2)
    send_far(0, near)

    arrived(m1r.at[1:4], m1_sem)
    heads = jnp.concatenate(
        [m1r[dz, half * 2 + k : half * 2 + k + 1, :] for half in range(2) for dz in range(4) for k in range(2)],
        axis=0,
    )
    holder = heads // ROWS
    local = lax.rem(heads, ROWS)
    before = jnp.where(iota((TILE, TILE), 0) < iota((TILE, TILE), 1), 1.0, 0.0).astype(BF16)
    marks = jnp.concatenate([onehot(32, holder[u : u + 1, :]) for u in range(16)], axis=0)
    earlier = dot(marks, before, (1, 0)) * marks.astype(F32)
    rank = jnp.concatenate(
        [jnp.sum(earlier[u * 32 : (u + 1) * 32], axis=0, keepdims=True) for u in range(16)], axis=0
    ).astype(jnp.int32)
    away_x = lax.rem(holder // 8 + 4 - my_x, 4)
    away_y = lax.rem(lax.rem(holder // 2, 4) + 4 - my_y, 4)
    away_c = lax.rem(lax.rem(holder, 2) + 2 - my_c, 2)
    within = rank + 8 * lax.rem(iota((16, TILE), 0), 2)
    dest = [away_x * 2 + away_c, away_y * 2 + away_c]
    line_row = [away_y, away_x]
    slots = [dest[axis] * 64 + line_row[axis] * 16 + within for axis in range(2)]
    meta_row = [dest[axis] * 8 + line_row[axis] for axis in range(2)]
    meta_lane = within + 16 * (iota((16, TILE), 0) // 2)

    def pair(array, unit):
        return jnp.concatenate([array[2 * unit : 2 * unit + 1, :], array[2 * unit + 1 : 2 * unit + 2, :]], axis=1)

    live_z = m1r[0, 4:5, :] + m1r[1, 4:5, :] + m1r[2, 4:5, :] + m1r[3, 4:5, :]
    live_row = jnp.where(lax.rem(iota((64, TILE), 0), 8) == 4, live_z.astype(F32), 0.0)
    for axis in range(2):
        meta = live_row
        for unit in range(8):
            left = jnp.where(iota((64, 256), 0) == pair(meta_row[axis], unit), pair(local, unit).astype(F32), 0.0)
            meta = meta + dot(left.astype(BF16), onehot(TILE, pair(meta_lane, unit)), (1, 1))
        for d in range(8):
            target = m2s.at[axis, d] if d else m2r.at[axis, 0]
            target[...] = meta[d * 8 : (d + 1) * 8, :]
        for d in range(1, 8):
            remote(m2s.at[axis, d], m2r.at[axis, d], m2_sem, line(axis, d))


    forward(0, 0)
    compute(3)
    near = send_tiles(1)
    forward(1, 0)
    relay(0, 1)
    relay(0, 3)
    send_far(1, near)
    relay(0, 2)

    for dz in (1, 3, 2):
        relay(1, dz)

    arrived(m2r.at[:, 1:8], m2_sem)
    live_x = m2r[0, 0, 4:5, :]
    for d in range(1, 8):
        live_x = live_x + m2r[0, d, 4:5, :]
    live_x = jnp.broadcast_to(live_x, (8, TILE))
    m3r[0] = live_x
    m3s[...] = live_x
    for dy in (1, 2, 3):
        remote(m3s, m3r.at[dy], m3_sem, device(dy=dy))

    low = iota((8, TILE), 1) < 64
    for half in range(2):
        for axis in range(2):
            index = []
            for d in range(0, 8, 2):
                a, b = m2r[axis, d], m2r[axis, d + 1]
                if half == 0:
                    index.append(jnp.where(low, a, pltpu.roll(b, 64, 1)))
                else:
                    index.append(jnp.where(low, pltpu.roll(a, 64, 1), b))
            index = jnp.concatenate(index, axis=1).astype(jnp.int32)
            for row in range(4):
                hot[half, axis, row] = onehot(ROWS, index[row : row + 1, :])

    for half in range(2):
        for dz in ((0, 1, 3, 2) if half == 0 else (0, 1, 3, 2)):
            arrived(sr.at[half, :, 1:8, dz], s_sem.at[half * 4 + dz])
        for row in (1, 2, 3, 0):
            for axis in range(2):
                data = sr[half, axis, :, :, row].reshape(512, HEAD)
                part = dot(hot[half, axis, row], data, (1, 0))
                if half == 0:
                    acc[axis, row] = part
                elif row == 0:
                    acc[axis, 0] = acc[axis, 0] + part
                else:
                    ds_[axis, row] = (acc[axis, row] + part).astype(BF16)
            if half == 1 and row == 3:
                for away in (2, 1, 3):
                    remote(ds_.at[0, away], dr.at[0, away], d_sem, device(dy=away))
                    remote(ds_.at[1, away], dr.at[1, away], d_sem, device(dx=away))

    arrived(m3r.at[1:4], m3_sem)
    total_live = m3r[0] + m3r[1] + m3r[2] + m3r[3]
    factor = (float(SEQ * 4 * 128) / total_live)[:1]
    arrived(dr.at[:, 1:4], d_sem)
    for axis in range(2):
        result = acc[axis, 0]
        for row in range(1, 4):
            result = result + dr[axis, row].astype(F32)
        out_ref[:, axis * HEAD : (axis + 1) * HEAD] = result * factor
    for copy in sent:
        copy.wait_send()


def on_device(embeds, out_grad, w_query, w_key, w_value, lengths, item_rows, tile_owner):
    vmem = pl.BlockSpec(memory_space=pltpu.VMEM)
    smem = pl.BlockSpec(memory_space=pltpu.SMEM)
    width = 2 * HEAD
    total = pl.pallas_call(
        kernel,
        out_shape=pltpu.VMEM((ROWS, width), F32),
        in_specs=[smem, smem] + [pl.BlockSpec(memory_space=pl.ANY)] * 6,
        out_specs=vmem,
        scratch_shapes=[
            pltpu.VMEM((16, TILE), jnp.int32),
            pltpu.VMEM((4 * SEQ, width), BF16),
            pltpu.VMEM((4 * SEQ, width), BF16),
            pltpu.VMEM((width, width), BF16),
            pltpu.VMEM((width, width), BF16),
            pltpu.VMEM((width, width), BF16),
            pltpu.SemaphoreType.DMA((5,)),
            pltpu.VMEM((16, TILE, 2 * HEAD), BF16),
            pltpu.SMEM((16,), jnp.int32),
            pltpu.VMEM((4, 8, TILE), jnp.int32),
            pltpu.VMEM((4, 8, TILE), jnp.int32),
            pltpu.VMEM((2, 4, 2 * TILE, 2 * HEAD), BF16),
            pltpu.VMEM((2, 4, 2 * TILE, 2 * HEAD), BF16),
            pltpu.VMEM((2, 8, 8, TILE), F32),
            pltpu.VMEM((2, 8, 8, TILE), F32),
            pltpu.VMEM((2, 2, 8, 4, 4, 16, HEAD), BF16),
            pltpu.VMEM((2, 2, 8, 4, 4, 16, HEAD), BF16),
            pltpu.VMEM((8, TILE), F32),
            pltpu.VMEM((4, 8, TILE), F32),
            pltpu.VMEM((2, 2, 4, ROWS, 512), BF16),
            pltpu.VMEM((2, 4, ROWS, HEAD), F32),
            pltpu.VMEM((2, 4, ROWS, HEAD), BF16),
            pltpu.VMEM((2, 4, ROWS, HEAD), BF16),
            pltpu.SemaphoreType.DMA(()),
            pltpu.SemaphoreType.DMA((2,)),
            pltpu.SemaphoreType.DMA(()),
            pltpu.SemaphoreType.DMA((8,)),
            pltpu.SemaphoreType.DMA(()),
            pltpu.SemaphoreType.DMA((8,)),
            pltpu.SemaphoreType.DMA(()),
            pltpu.SemaphoreType.DMA(()),
        ],
        compiler_params=pltpu.CompilerParams(
            collective_id=0, has_side_effects=True, vmem_limit_bytes=60 << 20,
        ),
        name="gated_attention_table_grad",
    )(
        lengths,
        tile_owner,
        item_rows.reshape(-1, TILE),
        embeds,
        out_grad,
        w_query,
        w_key,
        w_value,
    )
    return total


def solution(mesh):
    both = ("group", "batch")
    placed = (P(both, None), P(both, None), P(), P(), P(), P(both), P(both), P(both))
    return jax.shard_map(
        on_device, mesh=mesh, in_specs=placed, out_specs=P(both, None), check_vma=False
    )
```

```python
import functools
import math

import jax
import jax.numpy as jnp
from jax import lax
from jax.experimental import pallas as pl
from jax.experimental.pallas import tpu as pltpu
from jax.sharding import PartitionSpec as P

SEQ = 512
TILE = 128
HEAD = 128
BLOCK = 128
ROWS = 256
MESH_ID = pl.DeviceIdType.MESH
F32 = jnp.float32
BF16 = jnp.bfloat16


def dot(a, b, dims):
    return lax.dot_general(a, b, ((dims[:1], dims[1:]), ((), ())), preferred_element_type=F32)


def iota(shape, dim):
    return lax.broadcasted_iota(jnp.int32, shape, dim)


def onehot(rows, index):
    return jnp.where(iota((rows, index.shape[1]), 0) == index, 1.0, 0.0).astype(BF16)


def gate(raw, attend_grad, weight):
    half = raw * (0.5 / math.sqrt(HEAD))
    tanh = jnp.tanh(half)
    gated = (1.0 + tanh) * weight
    attend = half * gated
    score = (attend_grad * gated) * (1.0 + half * (1.0 - tanh))
    return attend.astype(BF16), score.astype(BF16)


def history(item, len_ref, emb, grad, wq, wk, wv, tok_ref):
    span = pl.ds(item * SEQ, SEQ)
    embeds, grads = emb[span, :], grad[span, :]
    query = dot(embeds, wq[...], (1, 0)).astype(BF16)
    keys = dot(embeds, wk[...], (1, 0)).astype(BF16)
    value = dot(embeds, wv[...], (1, 0)).astype(BF16)
    counts = jnp.full((1, SEQ), len_ref[item], jnp.int32)
    weight = jnp.where(iota((1, SEQ), 1) < counts, 1.0 / counts.astype(F32), 0.0)
    causal = iota((BLOCK, BLOCK), 1) >= iota((BLOCK, BLOCK), 0)
    empty = jnp.zeros((BLOCK, BLOCK), BF16)
    wide = 2 * BLOCK
    parts = [[], [], []]
    for head in range(2):
        cols = slice(head * HEAD, (head + 1) * HEAD)
        totals = [[None, None], [None, None], [None, None]]

        def add(which, block, piece):
            old = totals[which][block]
            totals[which][block] = piece if old is None else old + piece

        for j, i in ((0, 1), (0, 0), (1, 1)):
            rows, others = slice(j * wide, (j + 1) * wide), slice(i * wide, (i + 1) * wide)
            k, v, q, g = keys[rows, cols], value[rows, cols], query[others, cols], grads[others, cols]
            raw = dot(k, q, (1, 1))
            attend_grad = dot(v, g, (1, 1))
            w = weight[:, others]
            if j == i:
                first = jnp.where(causal, w[:, :BLOCK], 0.0)
                last = jnp.where(causal, w[:, BLOCK:], 0.0)
                rest = jnp.broadcast_to(w[:, BLOCK:], (BLOCK, BLOCK))
                upper = gate(raw[:BLOCK], attend_grad[:BLOCK], jnp.concatenate([first, rest], axis=1))
                lower = gate(raw[BLOCK:, BLOCK:], attend_grad[BLOCK:, BLOCK:], last)
                attend, score = (
                    jnp.concatenate([a, jnp.concatenate([empty, b], axis=1)], axis=0)
                    for a, b in zip(upper, lower)
                )
            else:
                attend, score = gate(raw, attend_grad, w)
            add(2, j, dot(attend, g, (1, 0)))
            add(1, j, dot(score, q, (1, 0)))
            add(0, i, dot(score, k, (0, 0)))
        scales = (0.5 / math.sqrt(HEAD), 0.5 / math.sqrt(HEAD), None)
        for which in range(3):
            whole = jnp.concatenate(totals[which], axis=0)
            if scales[which] is not None:
                whole = whole * scales[which]
            parts[which].append(whole.astype(BF16))
    token = None
    for which, w in enumerate((wq, wk, wv)):
        piece = dot(jnp.concatenate(parts[which], axis=1), w[...], (1, 1))
        token = piece if token is None else token + piece
    tiles = SEQ // TILE
    tok_ref[pl.ds(item * tiles, tiles)] = token.astype(BF16).reshape(tiles, TILE, 2 * HEAD)


def kernel(
    len_ref, owner_ref, rows_hbm, emb_hbm, og_hbm, wq_hbm, wk_hbm, wv_hbm, out_ref,
    rows_ref, emb, grad, wq, wk, wv, in_sem,
    tok, order, m1s, m1r, zs, zr, m2s, m2r, ss, sr, m3s, m3r, hot, acc, ds_, dr,
    send_sem, near_sem, m1_sem, z_sem, m2_sem, s_sem, m3_sem, d_sem,
):
    group = lax.axis_index("group")
    batch = lax.axis_index("batch")
    my_x, my_y, my_c = batch // 8, lax.rem(batch // 2, 4), lax.rem(batch, 2)

    def device(dx=0, dy=0, dz=0, dc=0):
        x, y = lax.rem(my_x + dx, 4), lax.rem(my_y + dy, 4)
        return (lax.rem(group + dz, 4), x * 8 + y * 2 + lax.rem(my_c + dc, 2))

    def line(axis, d):
        return device(dx=d // 2, dc=d % 2) if axis == 0 else device(dy=d // 2, dc=d % 2)

    loads = [[] for _ in range(5)]

    def load(stage, source, target):
        copy = pltpu.make_async_copy(source, target, in_sem.at[stage])
        copy.start()
        loads[stage].append(copy)

    for source, target in ((wq_hbm, wq), (wk_hbm, wk), (wv_hbm, wv), (rows_hbm, rows_ref)):
        load(0, source, target)
    for item in range(4):
        span = pl.ds(item * SEQ, SEQ)
        load(item + 1 if item else 0, emb_hbm.at[span, :], emb.at[span, :])
        load(item + 1 if item else 0, og_hbm.at[span, :], grad.at[span, :])

    peers = [device(dz=d) for d in (1, 2, 3)]
    peers += [line(0, d) for d in range(1, 8)] + [line(1, d) for d in range(2, 8)]
    barrier = pltpu.get_barrier_semaphore()
    for peer in peers:
        pl.semaphore_signal(barrier, inc=1, device_id=peer, device_id_type=MESH_ID)

    sent = []

    def remote(source, target, sem, peer, left=None):
        copy = pltpu.make_async_remote_copy(
            src_ref=source,
            dst_ref=target,
            send_sem=send_sem if left is None else left,
            recv_sem=sem,
            device_id=peer,
            device_id_type=MESH_ID,
        )
        copy.start()
        if left is None:
            sent.append(copy)
        return copy

    def arrived(target, sem):
        pltpu.make_async_copy(target, target, sem).wait()

    live = len_ref[0] + len_ref[1] + len_ref[2] + len_ref[3]
    for half in range(2):
        owner = [owner_ref[half * 8 + t] for t in range(8)]
        place = []
        for t in range(8):
            at = 2 * owner[t]
            for other in owner[:t]:
                at = at + jnp.where(other == owner[t], 1, 0)
            place.append(at)
        for p in range(8):
            tile = 0
            for t in range(1, 8):
                tile = tile + jnp.where(place[t] == p, t, 0)
            order[half * 8 + p] = tile + half * 8

    def owned(half, dz, k):
        return order[half * 8 + 2 * lax.rem(group + dz, 4) + k]

    def compute(item):
        for copy in loads[item + 1 if item else 0]:
            copy.wait()
        history(item, len_ref, emb, grad, wq, wk, wv, tok)

    compute(0)
    pl.semaphore_wait(barrier, len(peers))
    for dz in range(4):
        target = m1s.at[dz] if dz else m1r.at[0]
        for half in range(2):
            for k in range(2):
                target[half * 2 + k : half * 2 + k + 1, :] = rows_ref[pl.ds(owned(half, dz, k), 1), :]
        target[4:5, :] = jnp.full((1, TILE), live, jnp.int32)
        target[5:8, :] = jnp.zeros((3, TILE), jnp.int32)
    for dz in range(1, 4):
        remote(m1s.at[dz], m1r.at[dz], m1_sem, device(dz=dz))

    def send_tiles(half):
        near = []
        for dz in (1, 3, 2):
            for k in range(2):
                zs[half, dz, pl.ds(k * TILE, TILE), :] = tok[owned(half, dz, k)]
            if dz != 2:
                left = near_sem.at[half]
                near.append(
                    remote(zs.at[half, dz], zr.at[half, dz], z_sem.at[half * 4 + dz], device(dz=dz), left)
                )
        for k in range(2):
            zr[half, 0, pl.ds(k * TILE, TILE), :] = tok[owned(half, 0, k)]
        return near

    def send_far(half, near):
        for copy in near:
            copy.wait_send()
        remote(zs.at[half, 2], zr.at[half, 2], z_sem.at[half * 4 + 2], device(dz=2))

    compute(1)
    near = send_tiles(0)

    def forward(half, dz):
        for axis in range(2):
            packed = dot(
                onehot(512, pair(slots[axis], half * 4 + dz)),
                zr[half, dz, :, axis * HEAD : (axis + 1) * HEAD],
                (1, 0),
            ).astype(BF16)
            for d in range(8):
                target = ss.at[half, axis, d, dz] if d else sr.at[half, axis, 0, dz]
                for row in range(4):
                    target[row] = packed[d * 64 + row * 16 : d * 64 + row * 16 + 16]
        for d in (4, 5, 2, 6, 3, 7, 1):
            for axis in range(2):
                remote(ss.at[half, axis, d, dz], sr.at[half, axis, d, dz], s_sem.at[half * 4 + dz], line(axis, d))

    def relay(half, dz):
        arrived(zr.at[half, dz], z_sem.at[half * 4 + dz])
        forward(half, dz)

    compute(2)
    send_far(0, near)
    compute(3)
    near = send_tiles(1)

    arrived(m1r.at[1:4], m1_sem)
    heads = jnp.concatenate(
        [m1r[dz, half * 2 + k : half * 2 + k + 1, :] for half in range(2) for dz in range(4) for k in range(2)],
        axis=0,
    )
    holder = heads // ROWS
    local = lax.rem(heads, ROWS)
    before = jnp.where(iota((TILE, TILE), 0) < iota((TILE, TILE), 1), 1.0, 0.0).astype(BF16)
    marks = jnp.concatenate([onehot(32, holder[u : u + 1, :]) for u in range(16)], axis=0)
    earlier = dot(marks, before, (1, 0)) * marks.astype(F32)
    rank = jnp.concatenate(
        [jnp.sum(earlier[u * 32 : (u + 1) * 32], axis=0, keepdims=True) for u in range(16)], axis=0
    ).astype(jnp.int32)
    away_x = lax.rem(holder // 8 + 4 - my_x, 4)
    away_y = lax.rem(lax.rem(holder // 2, 4) + 4 - my_y, 4)
    away_c = lax.rem(lax.rem(holder, 2) + 2 - my_c, 2)
    within = rank + 8 * lax.rem(iota((16, TILE), 0), 2)
    dest = [away_x * 2 + away_c, away_y * 2 + away_c]
    line_row = [away_y, away_x]
    slots = [dest[axis] * 64 + line_row[axis] * 16 + within for axis in range(2)]
    meta_row = [dest[axis] * 8 + line_row[axis] for axis in range(2)]
    meta_lane = within + 16 * (iota((16, TILE), 0) // 2)

    def pair(array, unit):
        return jnp.concatenate([array[2 * unit : 2 * unit + 1, :], array[2 * unit + 1 : 2 * unit + 2, :]], axis=1)

    live_z = m1r[0, 4:5, :] + m1r[1, 4:5, :] + m1r[2, 4:5, :] + m1r[3, 4:5, :]
    live_row = jnp.where(lax.rem(iota((64, TILE), 0), 8) == 4, live_z.astype(F32), 0.0)
    for axis in range(2):
        meta = live_row
        for unit in range(8):
            left = jnp.where(iota((64, 256), 0) == pair(meta_row[axis], unit), pair(local, unit).astype(F32), 0.0)
            meta = meta + dot(left.astype(BF16), onehot(TILE, pair(meta_lane, unit)), (1, 1))
        for d in range(8):
            target = m2s.at[axis, d] if d else m2r.at[axis, 0]
            target[...] = meta[d * 8 : (d + 1) * 8, :]
        for d in range(1, 8):
            remote(m2s.at[axis, d], m2r.at[axis, d], m2_sem, line(axis, d))


    forward(0, 0)
    forward(1, 0)
    relay(0, 1)
    relay(0, 3)
    send_far(1, near)
    relay(0, 2)

    for dz in (1, 3, 2):
        relay(1, dz)

    arrived(m2r.at[:, 1:8], m2_sem)
    live_x = m2r[0, 0, 4:5, :]
    for d in range(1, 8):
        live_x = live_x + m2r[0, d, 4:5, :]
    live_x = jnp.broadcast_to(live_x, (8, TILE))
    m3r[0] = live_x
    m3s[...] = live_x
    for dy in (1, 2, 3):
        remote(m3s, m3r.at[dy], m3_sem, device(dy=dy))

    low = iota((8, TILE), 1) < 64
    for half in range(2):
        for axis in range(2):
            index = []
            for d in range(0, 8, 2):
                a, b = m2r[axis, d], m2r[axis, d + 1]
                if half == 0:
                    index.append(jnp.where(low, a, pltpu.roll(b, 64, 1)))
                else:
                    index.append(jnp.where(low, pltpu.roll(a, 64, 1), b))
            index = jnp.concatenate(index, axis=1).astype(jnp.int32)
            for row in range(4):
                hot[half, axis, row] = onehot(ROWS, index[row : row + 1, :])

    for half in range(2):
        for dz in ((0, 1, 3, 2) if half == 0 else (0, 1, 3, 2)):
            arrived(sr.at[half, :, 1:8, dz], s_sem.at[half * 4 + dz])
        for row in (1, 2, 3, 0):
            for axis in range(2):
                data = sr[half, axis, :, :, row].reshape(512, HEAD)
                part = dot(hot[half, axis, row], data, (1, 0))
                if half == 0:
                    acc[axis, row] = part
                elif row == 0:
                    acc[axis, 0] = acc[axis, 0] + part
                else:
                    ds_[axis, row] = (acc[axis, row] + part).astype(BF16)
            if half == 1 and row == 3:
                for away in (2, 1, 3):
                    remote(ds_.at[0, away], dr.at[0, away], d_sem, device(dy=away))
                    remote(ds_.at[1, away], dr.at[1, away], d_sem, device(dx=away))

    arrived(m3r.at[1:4], m3_sem)
    total_live = m3r[0] + m3r[1] + m3r[2] + m3r[3]
    factor = (float(SEQ * 4 * 128) / total_live)[:1]
    arrived(dr.at[:, 1:4], d_sem)
    for axis in range(2):
        result = acc[axis, 0]
        for row in range(1, 4):
            result = result + dr[axis, row].astype(F32)
        out_ref[:, axis * HEAD : (axis + 1) * HEAD] = result * factor
    for copy in sent:
        copy.wait_send()


def on_device(embeds, out_grad, w_query, w_key, w_value, lengths, item_rows, tile_owner):
    vmem = pl.BlockSpec(memory_space=pltpu.VMEM)
    smem = pl.BlockSpec(memory_space=pltpu.SMEM)
    width = 2 * HEAD
    total = pl.pallas_call(
        kernel,
        out_shape=pltpu.VMEM((ROWS, width), F32),
        in_specs=[smem, smem] + [pl.BlockSpec(memory_space=pl.ANY)] * 6,
        out_specs=vmem,
        scratch_shapes=[
            pltpu.VMEM((16, TILE), jnp.int32),
            pltpu.VMEM((4 * SEQ, width), BF16),
            pltpu.VMEM((4 * SEQ, width), BF16),
            pltpu.VMEM((width, width), BF16),
            pltpu.VMEM((width, width), BF16),
            pltpu.VMEM((width, width), BF16),
            pltpu.SemaphoreType.DMA((5,)),
            pltpu.VMEM((16, TILE, 2 * HEAD), BF16),
            pltpu.SMEM((16,), jnp.int32),
            pltpu.VMEM((4, 8, TILE), jnp.int32),
            pltpu.VMEM((4, 8, TILE), jnp.int32),
            pltpu.VMEM((2, 4, 2 * TILE, 2 * HEAD), BF16),
            pltpu.VMEM((2, 4, 2 * TILE, 2 * HEAD), BF16),
            pltpu.VMEM((2, 8, 8, TILE), F32),
            pltpu.VMEM((2, 8, 8, TILE), F32),
            pltpu.VMEM((2, 2, 8, 4, 4, 16, HEAD), BF16),
            pltpu.VMEM((2, 2, 8, 4, 4, 16, HEAD), BF16),
            pltpu.VMEM((8, TILE), F32),
            pltpu.VMEM((4, 8, TILE), F32),
            pltpu.VMEM((2, 2, 4, ROWS, 512), BF16),
            pltpu.VMEM((2, 4, ROWS, HEAD), F32),
            pltpu.VMEM((2, 4, ROWS, HEAD), BF16),
            pltpu.VMEM((2, 4, ROWS, HEAD), BF16),
            pltpu.SemaphoreType.DMA(()),
            pltpu.SemaphoreType.DMA((2,)),
            pltpu.SemaphoreType.DMA(()),
            pltpu.SemaphoreType.DMA((8,)),
            pltpu.SemaphoreType.DMA(()),
            pltpu.SemaphoreType.DMA((8,)),
            pltpu.SemaphoreType.DMA(()),
            pltpu.SemaphoreType.DMA(()),
        ],
        compiler_params=pltpu.CompilerParams(
            collective_id=0, has_side_effects=True, vmem_limit_bytes=60 << 20,
        ),
        name="gated_attention_table_grad",
    )(
        lengths,
        tile_owner,
        item_rows.reshape(-1, TILE),
        embeds,
        out_grad,
        w_query,
        w_key,
        w_value,
    )
    return total


def solution(mesh):
    both = ("group", "batch")
    placed = (P(both, None), P(both, None), P(), P(), P(), P(both), P(both), P(both))
    return jax.shard_map(
        on_device, mesh=mesh, in_specs=placed, out_specs=P(both, None), check_vma=False
    )
```
